32 devices in a mesh: groups: 2 (over y), frame: 16 (over z, x, core).
Axes of the slice: x: 2, y: 2, z: 4, core: 2. Of those that a mesh axis runs over, the one named last changes fastest.
Arguments:
- queries: bfloat16 [8192, 1536], P(('groups', 'frame')), parts along dimension 0, may hold values from -14 to 14
- key_heads: bfloat16 [8192, 1536], P(('groups', 'frame')), parts along dimension 0, may hold values from -14 to 14
- value_heads: bfloat16 [8192, 1536], P(('groups', 'frame')), parts along dimension 0, may hold values from -6 to 6
- tile_lists: int32 [16, 8], P('frame'), may hold values from 0 to 1
Outputs:
- attended: bfloat16 [8192, 1536], P(('groups', 'frame')), parts along dimension 0
The draws below stay inside these ranges and needn't reach their ends.
There are 2 independent parts, one for each index of `groups`. The reference program is written for one: setup_inputs(seed, part) draws one part's arguments, and reference() takes and returns one part's arrays. A program takes and returns all parts, laid end to end along the dimension named above; an argument that names none is the same for every part. Nothing has to cross between parts.
Inputs may be any that keep to these rules, and one draw needn't show every extreme that they name: `tile_lists`: entry l of a frame's row names a block of the frame 2^l before it, entry 4 + l one of the frame 2^l after it; entries for frames outside the video are not read.
All inputs are finite; a program needn't handle non-finite values.
Results may differ from the reference program's by a relative error of at most 0.0049.
Values may be sent and summed in bfloat16 or wider, within the bound.
A program may use at most 64 MiB of HBM per device.

```python
import math
import jax
import jax.numpy as jnp
from jax import lax

HEADS = 12
HD = 128
TILE = 128
TF = 2
LEVELS = 4
FRAMES = 16
TOKENS = 4096
HC = 1536


def pair_draw(key):
    shape = (TOKENS, HEADS * HD)
    query_base = 1.4 * jnp.clip(jax.random.normal(jax.random.fold_in(key, 11), shape, jnp.float32), -4.0, 4.0)
    key_base = 1.4 * jnp.clip(jax.random.normal(jax.random.fold_in(key, 12), shape, jnp.float32), -4.0, 4.0)
    return (query_base, key_base)


def draw_queries(key, part):
    return pair_draw(key)[0].astype(jnp.bfloat16)


def draw_key_heads(key, part):
    return pair_draw(key)[1].astype(jnp.bfloat16)


def place_ends(entries, stream_key, smallest, high):
    longest = entries.shape.index(max(entries.shape))
    spots = []
    for shift in (0, 1):
        where = [jax.random.randint(jax.random.fold_in(stream_key, axis), (), 0, length) for axis, length in enumerate(entries.shape)]
        where[longest] = (where[longest] + shift) % entries.shape[longest]
        spots.append(tuple(where))
    return entries.at[spots[0]].set(smallest).at[spots[1]].set(high)


def steps_of(rng, shape, split, least, largest):
    def one(dim, blocks):
        heights = jax.random.uniform(jax.random.fold_in(jax.random.fold_in(rng, 6), dim), (blocks,), jnp.float32, least / len(split), largest / len(split))
        return jnp.repeat(jnp.exp(heights), shape[dim] // blocks).reshape((-1,) + (1,) * (len(shape) - dim - 1))

    gain = one(*split[0])
    for cut in split[1:]:
        gain = gain * one(*cut)
    return gain


def centred(key, dims, scale, bound, shards=(), kind=jnp.bfloat16):
    result = scale * jax.random.normal(key, dims, jnp.float32)
    if shards:
        result = result * steps_of(key, dims, shards, -0.22, 0.18)
    return jnp.clip(result, -bound, bound).astype(kind)


def setup_inputs(seed: int = 0, part: int = 0) -> dict:
    seeds = jax.random.split(jax.random.key(seed), 5)
    own_keys = jax.random.split(jax.random.fold_in(seeds[4], part), 5)
    return {
        "queries": draw_queries(jax.random.fold_in(jax.random.fold_in(seeds[4], part), 71), part),
        "key_heads": draw_key_heads(jax.random.fold_in(jax.random.fold_in(seeds[4], part), 71), part),
        "value_heads": centred(own_keys[2], (TOKENS, HC), 1.5, 6.0, ((0, 16),)),
        "tile_lists": place_ends(jax.random.randint(seeds[3], (FRAMES, 2 * LEVELS), 0, TF), jax.random.fold_in(seeds[3], 1), 0, TF - 1).astype(jnp.int32),
    }


def attend_block(block_queries, block_keys, block_values, usable):
    scale = 1.0 / math.sqrt(HD)

    def one_head(head):
        offset = head * HD
        head_queries = lax.dynamic_slice_in_dim(block_queries, offset, HD, 1)
        head_keys = lax.dynamic_slice_in_dim(block_keys, offset, HD, 1)
        head_values = lax.dynamic_slice_in_dim(block_values, offset, HD, 1)
        scores = lax.dot_general(head_queries, head_keys, (((1,), (1,)), ((), ())), preferred_element_type=jnp.float32) * scale
        scores = jnp.where(usable[None, :], scores, -jnp.inf)
        peak = lax.optimization_barrier(jnp.max(scores, axis=1, keepdims=True))
        raised = jnp.exp(scores - peak)
        weights = (raised / lax.optimization_barrier(jnp.sum(raised, axis=1, keepdims=True))).astype(jnp.bfloat16)
        return jnp.dot(weights, head_values, preferred_element_type=jnp.float32).astype(jnp.bfloat16)
    per_head = lax.map(one_head, jnp.arange(HEADS, dtype=jnp.int32))
    return jnp.transpose(per_head, (1, 0, 2)).reshape(block_queries.shape[0], HEADS * HD)

def reference(queries, key_heads, value_heads, tile_lists):
    frame_len = TF * TILE
    width = HEADS * HD
    query_frames = queries.reshape(FRAMES, frame_len, width)
    key_frames = key_heads.reshape(FRAMES, frame_len, width)
    value_frames = value_heads.reshape(FRAMES, frame_len, width)

    def per_frame(frame_no):
        own_queries = lax.dynamic_index_in_dim(query_frames, frame_no, 0, keepdims=False)
        own_lists = lax.dynamic_index_in_dim(tile_lists, frame_no, 0, keepdims=False)
        key_parts = [lax.dynamic_index_in_dim(key_frames, frame_no, 0, keepdims=False)]
        value_parts = [lax.dynamic_index_in_dim(value_frames, frame_no, 0, keepdims=False)]
        usable_parts = [jnp.ones((frame_len,), dtype=bool)]
        for upward in (0, 1):
            for level in range(LEVELS):
                distance = 2 ** level
                if upward:
                    source = frame_no + distance
                else:
                    source = frame_no - distance
                inside = (source >= 0) & (source < FRAMES)
                clipped = jnp.clip(source, 0, FRAMES - 1).astype(jnp.int32)
                first_row = (own_lists[upward * LEVELS + level] * TILE).astype(jnp.int32)
                start_index = (clipped, first_row, jnp.int32(0))
                key_parts.append(lax.dynamic_slice(key_frames, start_index, (1, TILE, width))[0])
                value_parts.append(lax.dynamic_slice(value_frames, start_index, (1, TILE, width))[0])
                usable_parts.append(jnp.broadcast_to(inside, (TILE,)))
        return attend_block(own_queries, jnp.concatenate(key_parts, axis=0), jnp.concatenate(value_parts, axis=0), jnp.concatenate(usable_parts, axis=0))
    attended = lax.map(per_frame, jnp.arange(FRAMES, dtype=jnp.int32))
    return attended.reshape(FRAMES * frame_len, width)
```

```python
import functools
import math

import jax
import jax.numpy as jnp
from jax import lax
from jax.experimental import pallas as pl
from jax.experimental.pallas import tpu as pltpu
from jax.sharding import PartitionSpec as P

HD = 128
TILE = 128
CHUNKS = 2
MESH = pl.DeviceIdType.MESH

CORE, ACROSS, ACROSS_RELAYED, MIRROR, BELOW8, ABOVE8 = range(6)
NEAR = 6


def kernel(n, levels, heads, *refs):
    q_ref, k_ref, v_ref, own_list, list_ref, out_ref = refs[:6]
    w_low = refs[6 : 6 + CHUNKS]
    w_high = refs[6 + CHUNKS : 6 + 2 * CHUNKS]
    (stage, landed, lists_v, lists_s, top, total, acc,
     w_send, w_recv, t_send, t_recv, l_send, l_recv, s_sem) = refs[6 + 2 * CHUNKS :]
    me = lax.axis_index("frame")
    quarter = me % 4
    x = quarter // 2
    core = me % 2
    core_peer = me + 1 - 2 * core
    across = me + 2 - 4 * x
    mirror = me + 3 - 2 * quarter
    has_low, has_high = me >= 4, me + 4 < n
    per = heads // CHUNKS
    width = per * HD
    far = [1 << level for level in range(4, levels)]
    yes = me >= 0

    partners = [
        (core_peer, yes, 0, 0),
        (across, yes, 1, 1),
        (mirror, yes, 2, 2),
        (me - 4, has_low, 3, 4),
        (me + 4, has_high, 4, 3),
    ]
    for j, d in enumerate(far):
        partners.append((me - d, me >= d, 5 + 2 * j, 6 + 2 * j))
        partners.append((me + d, me + d < n, 6 + 2 * j, 5 + 2 * j))

    barrier = pltpu.get_barrier_semaphore()
    for device, exists, _, _ in partners:
        @pl.when(exists)
        def _():
            pl.semaphore_signal(barrier, inc=1, device_id={"frame": device}, device_id_type=MESH)
    pl.semaphore_wait(barrier, sum(jnp.where(exists, 1, 0) for _, exists, _, _ in partners))

    def list_copy(device, here, there):
        return pltpu.make_async_remote_copy(
            src_ref=list_ref, dst_ref=lists_v.at[there],
            send_sem=l_send.at[here], recv_sem=l_recv.at[there],
            device_id={"frame": device}, device_id_type=MESH)

    def list_wait(here):
        return pltpu.make_async_remote_copy(
            src_ref=list_ref, dst_ref=lists_v.at[here],
            send_sem=l_send.at[here], recv_sem=l_recv.at[here],
            device_id={"frame": core_peer}, device_id_type=MESH)

    for device, exists, here, there in partners:
        @pl.when(exists)
        def _():
            list_copy(device, here, there).start()

    def whole_copy(side, chunk, kv):
        source = (k_ref, v_ref)[kv]
        target = (w_low, w_high)[side][chunk]
        return pltpu.make_async_remote_copy(
            src_ref=source.at[:, :, pl.ds(chunk * width, width)], dst_ref=target.at[kv],
            send_sem=w_send.at[side, chunk, kv], recv_sem=w_recv.at[side, chunk, kv],
            device_id={"frame": me + 4 if side == 0 else me - 4}, device_id_type=MESH)

    sides = ((has_high, has_low), (has_low, has_high))
    for chunk in range(CHUNKS):
        for side in range(2):
            @pl.when(sides[side][0])
            def _():
                for kv in range(2):
                    whole_copy(side, chunk, kv).start()

    for _, exists, here, _ in partners:
        @pl.when(exists)
        def _():
            list_wait(here).wait_recv()
            pltpu.make_async_copy(lists_v.at[here], lists_s.at[here], s_sem.at[here]).start()
    for _, exists, here, _ in partners:
        @pl.when(exists)
        def _():
            pltpu.make_async_copy(lists_v.at[here], lists_s.at[here], s_sem.at[here]).wait()

    def tile_copy(slot, chunk, device):
        return pltpu.make_async_remote_copy(
            src_ref=stage.at[slot, chunk], dst_ref=landed.at[slot, chunk],
            send_sem=t_send.at[slot, chunk], recv_sem=t_recv.at[slot, chunk],
            device_id={"frame": device}, device_id_type=MESH)

    def stage_own(slot, chunk, wanted):
        stage[slot, chunk, 0] = k_ref[wanted, :, pl.ds(chunk * width, width)]
        stage[slot, chunk, 1] = v_ref[wanted, :, pl.ds(chunk * width, width)]

    def stage_whole(slot, chunk, whole, wanted):
        stage[slot, chunk, 0] = whole[chunk][0, wanted]
        stage[slot, chunk, 1] = whole[chunk][1, wanted]

    inner = (quarter == 1) | (quarter == 2)
    far_sends = []
    for j, d in enumerate(far):
        far_sends.append((NEAR + 2 * j, me + d, me + d < n, 6 + 2 * j, 4 + j))
        far_sends.append((NEAR + 2 * j + 1, me - d, me >= d, 5 + 2 * j, levels + 4 + j))

    for chunk in range(CHUNKS):
        stage_own(ACROSS, chunk, lists_s[1, 0, 1 + levels * x])
        stage_own(CORE, chunk, lists_s[0, 0, levels * core])
        @pl.when(inner)
        def _():
            stage_own(MIRROR, chunk, lists_s[2, 0, levels * (x)])
        for slot, _, exists, here, entry in far_sends:
            @pl.when(exists)
            def _():
                stage_own(slot, chunk, lists_s[here, 0, entry])
    for chunk in range(CHUNKS):
        tile_copy(CORE, chunk, core_peer).start()
        @pl.when(inner)
        def _():
            tile_copy(MIRROR, chunk, mirror).start()
        tile_copy(ACROSS, chunk, across).start()
        for slot, device, exists, _, _ in far_sends:
            @pl.when(exists)
            def _():
                tile_copy(slot, chunk, device).start()

    factor = math.log2(math.e) / math.sqrt(HD)

    def one_head(h, keys, values, first):
        columns = pl.ds(pl.multiple_of(h * HD, HD), HD)
        scores = lax.dot_general(
            q_ref[:, columns], keys, (((1,), (1,)), ((), ())), preferred_element_type=jnp.float32)
        peak = jnp.max(scores, axis=1, keepdims=True)
        if not first:
            old = top[h][:, :1]
            peak = jnp.maximum(old, peak)
        raised = jnp.exp2((scores - peak) * factor)
        added = jnp.sum(raised, axis=1, keepdims=True)
        mixed = jnp.dot(raised.astype(jnp.bfloat16), values, preferred_element_type=jnp.float32)
        if not first:
            fade = jnp.exp2((old - peak) * factor)
            added = added + fade * total[h][:, :1]
            mixed = mixed + fade * acc[h]
        top[h] = jnp.broadcast_to(peak, (peak.shape[0], HD))
        total[h] = jnp.broadcast_to(added, (peak.shape[0], HD))
        acc[h] = mixed

    def attend(chunk, load, first=False):
        def step(i, carry):
            for j in range(2):
                local = i * 2 + j
                keys, values = load(pl.ds(pl.multiple_of(local * HD, HD), HD))
                one_head(chunk * per + local, keys, values, first)
            return carry
        lax.fori_loop(0, per // 2, step, 0)

    def attend_own(chunk):
        def load(columns):
            columns = pl.ds(pl.multiple_of(columns.start + chunk * width, HD), HD)
            keys, values = k_ref[:, :, columns], v_ref[:, :, columns]
            return keys.reshape(-1, HD), values.reshape(-1, HD)
        attend(chunk, load, True)

    def attend_whole(side, chunk):
        wanted = own_list[0, 2 + levels * side]
        whole = (w_low, w_high)[side][chunk]
        attend(chunk, lambda columns: (whole[0, wanted, :, columns], whole[1, wanted, :, columns]))

    def attend_landed(slot, chunk, exists):
        @pl.when(exists)
        def _():
            tile_copy(slot, chunk, core_peer).wait_recv()
            attend(chunk, lambda columns: (landed[slot, chunk, 0, :, columns], landed[slot, chunk, 1, :, columns]))

    def wait_whole(chunk):
        for side in range(2):
            @pl.when(sides[side][1])
            def _():
                for kv in range(2):
                    whole_copy(side, chunk, kv).wait_recv()

    relays = [
        (ACROSS_RELAYED, across, (x == 0) & has_high, w_high, 1, levels + 1),
        (ACROSS_RELAYED, across, (x == 1) & has_low, w_low, 1, 1),
        (MIRROR, mirror, (quarter == 0) & has_high, w_high, 2, levels),
        (MIRROR, mirror, (quarter == 3) & has_low, w_low, 2, 0),
        (BELOW8, me + 4, has_low & has_high, w_low, 4, 3),
        (ABOVE8, me - 4, has_low & has_high, w_high, 3, levels + 3),
    ]

    def relay(chunk):
        for slot, _, exists, whole, here, entry in relays:
            @pl.when(exists)
            def _():
                stage_whole(slot, chunk, whole, lists_s[here, 0, entry])
        for slot, device, exists, _, _, _ in relays:
            @pl.when(exists)
            def _():
                tile_copy(slot, chunk, device).start()

    def attend_wholes(chunk):
        for side in range(2):
            @pl.when(sides[side][1])
            def _():
                attend_whole(side, chunk)

    relayed_across = ((x == 0) & has_low) | ((x == 1) & has_high)
    outer = ((quarter == 0) & has_low) | ((quarter == 3) & has_high)

    for chunk in range(CHUNKS):
        attend_own(chunk)
    for chunk in range(CHUNKS):
        wait_whole(chunk)
        relay(chunk)
        attend_landed(CORE, chunk, yes)
        attend_wholes(chunk)
        attend_landed(ACROSS, chunk, yes)
    for chunk in range(CHUNKS):
        for j, d in enumerate(far):
            attend_landed(NEAR + 2 * j, chunk, me >= d)
            attend_landed(NEAR + 2 * j + 1, chunk, me + d < n)
        attend_landed(MIRROR, chunk, inner | outer)
        attend_landed(BELOW8, chunk, me >= 8)
        attend_landed(ABOVE8, chunk, me + 8 < n)
        attend_landed(ACROSS_RELAYED, chunk, relayed_across)
        for local in range(per):
            h = chunk * per + local
            out_ref[:, pl.ds(h * HD, HD)] = (acc[h] / total[h]).astype(out_ref.dtype)

    for _, exists, here, _ in partners:
        @pl.when(exists)
        def _():
            list_wait(here).wait_send()
    for chunk in range(CHUNKS):
        for side in range(2):
            @pl.when(sides[side][0])
            def _():
                for kv in range(2):
                    whole_copy(side, chunk, kv).wait_send()
        sent = [(CORE, yes), (ACROSS, yes), (MIRROR, inner)]
        sent += [(slot, exists) for slot, _, exists, _, _ in far_sends]
        sent += [(slot, exists) for slot, _, exists, _, _, _ in relays]
        for slot, exists in sent:
            @pl.when(exists)
            def _():
                tile_copy(slot, chunk, core_peer).wait_send()


def solution(mesh):
    n = mesh.shape["frame"]

    def body(queries, key_heads, value_heads, tile_lists):
        rows, channels = queries.shape
        heads = channels // HD
        tiles = rows // TILE
        levels = tile_lists.shape[1] // 2
        far = max(levels - 4, 0)
        width = channels // CHUNKS
        slots = NEAR + 2 * far
        lists = 5 + 2 * far
        padded = jnp.pad(tile_lists, ((0, 7), (0, 128 - 2 * levels)))
        vmem = pl.BlockSpec(memory_space=pltpu.VMEM)
        dma = pltpu.SemaphoreType.DMA
        whole = pltpu.VMEM((2, tiles, TILE, width), jnp.bfloat16)
        return pl.pallas_call(
            functools.partial(kernel, n, levels, heads),
            out_shape=jax.ShapeDtypeStruct((rows, channels), jnp.bfloat16),
            in_specs=[vmem, vmem, vmem, pl.BlockSpec(memory_space=pltpu.SMEM), vmem],
            out_specs=vmem,
            scratch_shapes=[whole] * (2 * CHUNKS)
            + [
                pltpu.VMEM((slots, CHUNKS, 2, TILE, width), jnp.bfloat16),
                pltpu.VMEM((slots, CHUNKS, 2, TILE, width), jnp.bfloat16),
                pltpu.VMEM((lists, 8, 128), jnp.int32),
                pltpu.SMEM((lists, 8, 128), jnp.int32),
                pltpu.VMEM((heads, rows, HD), jnp.float32),
                pltpu.VMEM((heads, rows, HD), jnp.float32),
                pltpu.VMEM((heads, rows, HD), jnp.float32),
                dma((2, CHUNKS, 2)),
                dma((2, CHUNKS, 2)),
                dma((slots, CHUNKS)),
                dma((slots, CHUNKS)),
                dma((lists,)),
                dma((lists,)),
                dma((lists,)),
            ],
            compiler_params=pltpu.CompilerParams(
                collective_id=0, has_side_effects=True, vmem_limit_bytes=60 << 20
            ),
        )(
            queries,
            key_heads.reshape(tiles, TILE, channels),
            value_heads.reshape(tiles, TILE, channels),
            tile_lists,
            padded,
        )

    in_specs = (
        P(("groups", "frame"), None),
        P(("groups", "frame"), None),
        P(("groups", "frame"), None),
        P("frame", None),
    )
    return jax.shard_map(
        body, mesh=mesh, in_specs=in_specs, out_specs=P(("groups", "frame"), None), check_vma=False
    )
```

```python
import functools
import math

import jax
import jax.numpy as jnp
from jax import lax
from jax.experimental import pallas as pl
from jax.experimental.pallas import tpu as pltpu
from jax.sharding import PartitionSpec as P

HD = 128
TILE = 128
CHUNKS = 6
MESH = pl.DeviceIdType.MESH

CORE, ACROSS, ACROSS_RELAYED, MIRROR, BELOW8, ABOVE8 = range(6)
NEAR = 6


def kernel(n, levels, heads, *refs):
    q_ref, k_ref, v_ref, own_list, list_ref, out_ref = refs[:6]
    w_low = refs[6 : 6 + CHUNKS]
    w_high = refs[6 + CHUNKS : 6 + 2 * CHUNKS]
    (stage, landed, lists_v, lists_s, top, total, acc,
     w_send, w_recv, t_send, t_recv, l_send, l_recv, s_sem) = refs[6 + 2 * CHUNKS :]
    me = lax.axis_index("frame")
    quarter = me % 4
    x = quarter // 2
    core = me % 2
    core_peer = me + 1 - 2 * core
    across = me + 2 - 4 * x
    mirror = me + 3 - 2 * quarter
    has_low, has_high = me >= 4, me + 4 < n
    per = heads // CHUNKS
    width = per * HD
    far = [1 << level for level in range(4, levels)]
    yes = me >= 0

    partners = [
        (core_peer, yes, 0, 0),
        (across, yes, 1, 1),
        (mirror, yes, 2, 2),
        (me - 4, has_low, 3, 4),
        (me + 4, has_high, 4, 3),
    ]
    for j, d in enumerate(far):
        partners.append((me - d, me >= d, 5 + 2 * j, 6 + 2 * j))
        partners.append((me + d, me + d < n, 6 + 2 * j, 5 + 2 * j))

    barrier = pltpu.get_barrier_semaphore()
    for device, exists, _, _ in partners:
        @pl.when(exists)
        def _():
            pl.semaphore_signal(barrier, inc=1, device_id={"frame": device}, device_id_type=MESH)
    pl.semaphore_wait(barrier, sum(jnp.where(exists, 1, 0) for _, exists, _, _ in partners))

    def list_copy(device, here, there):
        return pltpu.make_async_remote_copy(
            src_ref=list_ref, dst_ref=lists_v.at[there],
            send_sem=l_send.at[here], recv_sem=l_recv.at[there],
            device_id={"frame": device}, device_id_type=MESH)

    def list_wait(here):
        return pltpu.make_async_remote_copy(
            src_ref=list_ref, dst_ref=lists_v.at[here],
            send_sem=l_send.at[here], recv_sem=l_recv.at[here],
            device_id={"frame": core_peer}, device_id_type=MESH)

    for device, exists, here, there in partners:
        @pl.when(exists)
        def _():
            list_copy(device, here, there).start()

    def whole_copy(side, chunk, kv):
        source = (k_ref, v_ref)[kv]
        target = (w_low, w_high)[side][chunk]
        return pltpu.make_async_remote_copy(
            src_ref=source.at[:, :, pl.ds(chunk * width, width)], dst_ref=target.at[kv],
            send_sem=w_send.at[side, chunk, kv], recv_sem=w_recv.at[side, chunk, kv],
            device_id={"frame": me + 4 if side == 0 else me - 4}, device_id_type=MESH)

    sides = ((has_high, has_low), (has_low, has_high))
    for chunk in range(CHUNKS):
        for side in range(2):
            @pl.when(sides[side][0])
            def _():
                for kv in range(2):
                    whole_copy(side, chunk, kv).start()

    for _, exists, here, _ in partners:
        @pl.when(exists)
        def _():
            list_wait(here).wait_recv()
            pltpu.make_async_copy(lists_v.at[here], lists_s.at[here], s_sem.at[here]).start()
    for _, exists, here, _ in partners:
        @pl.when(exists)
        def _():
            pltpu.make_async_copy(lists_v.at[here], lists_s.at[here], s_sem.at[here]).wait()

    def tile_copy(slot, chunk, device):
        return pltpu.make_async_remote_copy(
            src_ref=stage.at[slot, chunk], dst_ref=landed.at[slot, chunk],
            send_sem=t_send.at[slot, chunk], recv_sem=t_recv.at[slot, chunk],
            device_id={"frame": device}, device_id_type=MESH)

    def stage_own(slot, chunk, wanted):
        stage[slot, chunk, 0] = k_ref[wanted, :, pl.ds(chunk * width, width)]
        stage[slot, chunk, 1] = v_ref[wanted, :, pl.ds(chunk * width, width)]

    def stage_whole(slot, chunk, whole, wanted):
        stage[slot, chunk, 0] = whole[chunk][0, wanted]
        stage[slot, chunk, 1] = whole[chunk][1, wanted]

    inner = (quarter == 1) | (quarter == 2)
    far_sends = []
    for j, d in enumerate(far):
        far_sends.append((NEAR + 2 * j, me + d, me + d < n, 6 + 2 * j, 4 + j))
        far_sends.append((NEAR + 2 * j + 1, me - d, me >= d, 5 + 2 * j, levels + 4 + j))

    for chunk in range(CHUNKS):
        stage_own(ACROSS, chunk, lists_s[1, 0, 1 + levels * x])
        stage_own(CORE, chunk, lists_s[0, 0, levels * core])
        @pl.when(inner)
        def _():
            stage_own(MIRROR, chunk, lists_s[2, 0, levels * (x)])
        for slot, _, exists, here, entry in far_sends:
            @pl.when(exists)
            def _():
                stage_own(slot, chunk, lists_s[here, 0, entry])
    for chunk in range(CHUNKS):
        tile_copy(CORE, chunk, core_peer).start()
        @pl.when(inner)
        def _():
            tile_copy(MIRROR, chunk, mirror).start()
        tile_copy(ACROSS, chunk, across).start()
        for slot, device, exists, _, _ in far_sends:
            @pl.when(exists)
            def _():
                tile_copy(slot, chunk, device).start()

    factor = math.log2(math.e) / math.sqrt(HD)

    def one_head(h, keys, values, first):
        columns = pl.ds(pl.multiple_of(h * HD, HD), HD)
        scores = lax.dot_general(
            q_ref[:, columns], keys, (((1,), (1,)), ((), ())), preferred_element_type=jnp.float32)
        peak = jnp.max(scores, axis=1, keepdims=True)
        if not first:
            old = top[h][:, :1]
            peak = jnp.maximum(old, peak)
        raised = jnp.exp2((scores - peak) * factor)
        added = jnp.sum(raised, axis=1, keepdims=True)
        mixed = jnp.dot(raised.astype(jnp.bfloat16), values, preferred_element_type=jnp.float32)
        if not first:
            fade = jnp.exp2((old - peak) * factor)
            added = added + fade * total[h][:, :1]
            mixed = mixed + fade * acc[h]
        top[h] = jnp.broadcast_to(peak, (peak.shape[0], HD))
        total[h] = jnp.broadcast_to(added, (peak.shape[0], HD))
        acc[h] = mixed

    def attend(chunk, load, first=False):
        def step(i, carry):
            for j in range(2):
                local = i * 2 + j
                keys, values = load(pl.ds(pl.multiple_of(local * HD, HD), HD))
                one_head(chunk * per + local, keys, values, first)
            return carry
        lax.fori_loop(0, per // 2, step, 0)

    def attend_own(chunk):
        def load(columns):
            columns = pl.ds(pl.multiple_of(columns.start + chunk * width, HD), HD)
            keys, values = k_ref[:, :, columns], v_ref[:, :, columns]
            return keys.reshape(-1, HD), values.reshape(-1, HD)
        attend(chunk, load, True)

    def attend_whole(side, chunk):
        wanted = own_list[0, 2 + levels * side]
        whole = (w_low, w_high)[side][chunk]
        attend(chunk, lambda columns: (whole[0, wanted, :, columns], whole[1, wanted, :, columns]))

    def attend_landed(slot, chunk, exists):
        @pl.when(exists)
        def _():
            tile_copy(slot, chunk, core_peer).wait_recv()
            attend(chunk, lambda columns: (landed[slot, chunk, 0, :, columns], landed[slot, chunk, 1, :, columns]))

    def wait_whole(chunk):
        for side in range(2):
            @pl.when(sides[side][1])
            def _():
                for kv in range(2):
                    whole_copy(side, chunk, kv).wait_recv()

    relays = [
        (ACROSS_RELAYED, across, (x == 0) & has_high, w_high, 1, levels + 1),
        (ACROSS_RELAYED, across, (x == 1) & has_low, w_low, 1, 1),
        (MIRROR, mirror, (quarter == 0) & has_high, w_high, 2, levels),
        (MIRROR, mirror, (quarter == 3) & has_low, w_low, 2, 0),
        (BELOW8, me + 4, has_low & has_high, w_low, 4, 3),
        (ABOVE8, me - 4, has_low & has_high, w_high, 3, levels + 3),
    ]

    def relay(chunk):
        for slot, _, exists, whole, here, entry in relays:
            @pl.when(exists)
            def _():
                stage_whole(slot, chunk, whole, lists_s[here, 0, entry])
        for slot, device, exists, _, _, _ in relays:
            @pl.when(exists)
            def _():
                tile_copy(slot, chunk, device).start()

    def attend_wholes(chunk):
        for side in range(2):
            @pl.when(sides[side][1])
            def _():
                attend_whole(side, chunk)

    relayed_across = ((x == 0) & has_low) | ((x == 1) & has_high)
    outer = ((quarter == 0) & has_low) | ((quarter == 3) & has_high)

    for chunk in range(CHUNKS):
        attend_own(chunk)
    for chunk in range(CHUNKS):
        wait_whole(chunk)
        relay(chunk)
        attend_landed(CORE, chunk, yes)
        attend_wholes(chunk)
        attend_landed(ACROSS, chunk, yes)
    for chunk in range(CHUNKS):
        for j, d in enumerate(far):
            attend_landed(NEAR + 2 * j, chunk, me >= d)
            attend_landed(NEAR + 2 * j + 1, chunk, me + d < n)
        attend_landed(MIRROR, chunk, inner | outer)
        attend_landed(BELOW8, chunk, me >= 8)
        attend_landed(ABOVE8, chunk, me + 8 < n)
        attend_landed(ACROSS_RELAYED, chunk, relayed_across)
        for local in range(per):
            h = chunk * per + local
            out_ref[:, pl.ds(h * HD, HD)] = (acc[h] / total[h]).astype(out_ref.dtype)

    for _, exists, here, _ in partners:
        @pl.when(exists)
        def _():
            list_wait(here).wait_send()
    for chunk in range(CHUNKS):
        for side in range(2):
            @pl.when(sides[side][0])
            def _():
                for kv in range(2):
                    whole_copy(side, chunk, kv).wait_send()
        sent = [(CORE, yes), (ACROSS, yes), (MIRROR, inner)]
        sent += [(slot, exists) for slot, _, exists, _, _ in far_sends]
        sent += [(slot, exists) for slot, _, exists, _, _, _ in relays]
        for slot, exists in sent:
            @pl.when(exists)
            def _():
                tile_copy(slot, chunk, core_peer).wait_send()


def solution(mesh):
    n = mesh.shape["frame"]

    def body(queries, key_heads, value_heads, tile_lists):
        rows, channels = queries.shape
        heads = channels // HD
        tiles = rows // TILE
        levels = tile_lists.shape[1] // 2
        far = max(levels - 4, 0)
        width = channels // CHUNKS
        slots = NEAR + 2 * far
        lists = 5 + 2 * far
        padded = jnp.pad(tile_lists, ((0, 7), (0, 128 - 2 * levels)))
        vmem = pl.BlockSpec(memory_space=pltpu.VMEM)
        dma = pltpu.SemaphoreType.DMA
        whole = pltpu.VMEM((2, tiles, TILE, width), jnp.bfloat16)
        return pl.pallas_call(
            functools.partial(kernel, n, levels, heads),
            out_shape=jax.ShapeDtypeStruct((rows, channels), jnp.bfloat16),
            in_specs=[vmem, vmem, vmem, pl.BlockSpec(memory_space=pltpu.SMEM), vmem],
            out_specs=vmem,
            scratch_shapes=[whole] * (2 * CHUNKS)
            + [
                pltpu.VMEM((slots, CHUNKS, 2, TILE, width), jnp.bfloat16),
                pltpu.VMEM((slots, CHUNKS, 2, TILE, width), jnp.bfloat16),
                pltpu.VMEM((lists, 8, 128), jnp.int32),
                pltpu.SMEM((lists, 8, 128), jnp.int32),
                pltpu.VMEM((heads, rows, HD), jnp.float32),
                pltpu.VMEM((heads, rows, HD), jnp.float32),
                pltpu.VMEM((heads, rows, HD), jnp.float32),
                dma((2, CHUNKS, 2)),
                dma((2, CHUNKS, 2)),
                dma((slots, CHUNKS)),
                dma((slots, CHUNKS)),
                dma((lists,)),
                dma((lists,)),
                dma((lists,)),
            ],
            compiler_params=pltpu.CompilerParams(
                collective_id=0, has_side_effects=True, vmem_limit_bytes=60 << 20
            ),
        )(
            queries,
            key_heads.reshape(tiles, TILE, channels),
            value_heads.reshape(tiles, TILE, channels),
            tile_lists,
            padded,
        )

    in_specs = (
        P(("groups", "frame"), None),
        P(("groups", "frame"), None),
        P(("groups", "frame"), None),
        P("frame", None),
    )
    return jax.shard_map(
        body, mesh=mesh, in_specs=in_specs, out_specs=P(("groups", "frame"), None), check_vma=False
    )
```
